32 devices in a mesh: groups: 2 (over y), ctx: 8 (over z, x), pb: 2 (over core).
Axes of the slice: x: 2, y: 2, z: 4, core: 2. Of those that a mesh axis runs over, the one named last changes fastest.
Arguments:
- att_query: bfloat16 [4, 8, 36864], P(('groups', 'pb'), 'ctx'), parts along dimension 0, may hold values from -26 to 26
- latent_cache: bfloat16 [4096, 576], P(('groups', 'ctx')), parts along dimension 0, may hold values from -6 to 6
- index_query: bfloat16 [4, 8, 4096], P(('groups', 'pb')), parts along dimension 0, may hold values from -70 to 70
- index_weight: float32 [4, 8, 32], P(('groups', 'pb')), parts along dimension 0, may hold values from -4 to 4
- index_keys: bfloat16 [4096, 128], P(('groups', 'ctx')), parts along dimension 0, may hold values from -16 to 16
- selected: int32 [4, 8, 1024], P(('groups', 'pb'), 'ctx'), parts along dimension 0, may hold values from 0 to 2047, as said below
Outputs:
- attended: bfloat16 [4, 8, 32768], P(('groups', 'pb'), 'ctx'), parts along dimension 0
- log_share: float32 [4, 8], P(('groups', 'pb')), parts along dimension 0
The draws below stay inside these ranges and needn't reach their ends.
There are 2 independent parts, one for each index of `groups`. The reference program is written for one: setup_inputs(seed, part) draws one part's arguments, and reference() takes and returns one part's arrays. A program takes and returns all parts, laid end to end along the dimension named above; each array names one. Nothing has to cross between parts.
Inputs may be any that keep to these rules, and one draw needn't show every extreme that they name: `selected`: each query's 1024 positions are distinct, ascending, no later than its own position, and include its own position and the one before. In each query's list at most 256 positions fall in any aligned block of 256 keys, and in every draw some such block holds exactly 256 positions of every query.
All inputs are finite; a program needn't handle non-finite values.
Results may differ from the reference program's by a relative error of at most 0.01.
Values may be sent and summed in bfloat16 or wider, within the bound.
A program may use at most 64 MiB of HBM per device.

```python
import math
import jax
import jax.numpy as jnp
from jax import lax

HEADS = 64
LATENT = 512
ROPE = 64
IHEADS = 32
IWIDTH = 128
TOPK = 1024
KEY_DEV = 256
KEYS = 2048
QB = 8
QBLOCKS = 2
QUERIES = 16
CAP = 256


def index_weights(key):
    return jnp.clip(jax.random.normal(jax.random.fold_in(key, 3), (QUERIES, IHEADS), jnp.float32), -4.0, 4.0)


def draw_latent_cache(key, part):
    values = jnp.clip(jax.random.normal(jax.random.fold_in(key, 1), (KEYS, LATENT + ROPE), jnp.float32), -6.0, 6.0)
    return values.astype(jnp.bfloat16)


def draw_att_query(key, part):
    values = jnp.clip(jax.random.normal(jax.random.fold_in(key, 2), (QUERIES, HEADS, LATENT + ROPE), jnp.float32), -6.0, 6.0) * 1.5
    return values.reshape(QBLOCKS, QB, HEADS * (LATENT + ROPE)).astype(jnp.bfloat16)


def draw_index_weight(key, part):
    return index_weights(key).reshape(QBLOCKS, QB, IHEADS)


def draw_index_query(key, part):
    values = jnp.clip(jax.random.normal(jax.random.fold_in(key, 4), (QUERIES, IHEADS, IWIDTH), jnp.float32), -4.0, 4.0)
    spread = jnp.exp(jax.random.uniform(jax.random.fold_in(key, 5), (QUERIES, 1, 1), jnp.float32, math.log(0.6), math.log(6.0)))
    values = values * spread
    return values.reshape(QBLOCKS, QB, IHEADS * IWIDTH).astype(jnp.bfloat16)


def draw_index_keys(key, part):
    values = jnp.clip(jax.random.normal(jax.random.fold_in(key, 6), (KEYS, IWIDTH), jnp.float32), -4.0, 4.0)
    spread = jnp.exp(jax.random.uniform(jax.random.fold_in(key, 7), (KEYS, 1), jnp.float32, math.log(0.4), math.log(4.0)))
    values = values * spread
    return values.astype(jnp.bfloat16)


def draw_selected(key, part):
    shards = KEYS // KEY_DEV
    capacity = CAP
    full_key, multiple_key, picking_key = jax.random.split(jax.random.fold_in(key, 11), 3)
    full_shard = jax.random.randint(full_key, (), 0, shards - 1)
    multiples = jax.random.randint(multiple_key, (QUERIES, shards), 1, 5)
    query_keys = jax.random.split(picking_key, QUERIES)
    positions = KEYS - QUERIES + jnp.arange(QUERIES)
    shard_ids = jnp.arange(shards)
    starts = shard_ids * KEY_DEV
    offsets_in = jnp.arange(KEY_DEV)
    global_places = starts[:, None] + offsets_in[None, :]

    def one_query(position, multiple, query_key):
        available = jnp.clip(position - starts + 1, 0, KEY_DEV)
        required = (shard_ids == position // KEY_DEV).astype(jnp.int32) + (shard_ids == (position - 1) // KEY_DEV).astype(jnp.int32)
        is_full = shard_ids == full_shard
        room = jnp.where(is_full, 0, jnp.minimum(capacity, available) - required)
        weight = jnp.where(is_full, 0, (shard_ids + 1) * multiple)
        remaining = TOPK - capacity - jnp.sum(jnp.where(is_full, 0, required))
        portion = jnp.minimum(room, remaining * weight // jnp.sum(weight))
        leftover = remaining - jnp.sum(portion)
        spare_room = (room - portion)[::-1]
        before = jnp.cumsum(spare_room) - spare_room
        topping = jnp.clip(leftover - before, 0, spare_room)[::-1]
        counts = jnp.where(is_full, capacity, required + portion + topping)
        orders = jax.vmap(lambda shard_key: jax.random.permutation(shard_key, KEY_DEV))(jax.random.split(query_key, shards))
        ranking = jnp.where(global_places == position, -2, jnp.where(global_places == position - 1, -1, jnp.where(global_places <= position, orders, KEY_DEV + offsets_in[None, :])))
        rank_of = jnp.argsort(jnp.argsort(ranking, axis=1, stable=True), axis=1, stable=True)
        chosen = rank_of < counts[:, None]
        order_score = jnp.where(chosen, KEYS - global_places, -1 - global_places).reshape(-1)
        values, unused = lax.top_k(order_score, TOPK)
        return (KEYS - values).astype(jnp.int32)
    selections = jax.vmap(one_query)(positions, multiples, query_keys)
    return selections.reshape(QBLOCKS, QB, TOPK)


def setup_inputs(seed: int = 0, part: int = 0) -> dict:
    arg_keys = jax.random.split(jax.random.key(seed), 7)
    part_splits = jax.random.split(jax.random.fold_in(arg_keys[6], part), 7)
    return {
        "att_query": draw_att_query(jax.random.fold_in(jax.random.fold_in(arg_keys[6], part), 71), part),
        "latent_cache": draw_latent_cache(jax.random.fold_in(jax.random.fold_in(arg_keys[6], part), 71), part),
        "index_query": draw_index_query(jax.random.fold_in(jax.random.fold_in(arg_keys[6], part), 71), part),
        "index_weight": draw_index_weight(jax.random.fold_in(jax.random.fold_in(arg_keys[6], part), 71), part),
        "index_keys": draw_index_keys(jax.random.fold_in(jax.random.fold_in(arg_keys[6], part), 71), part),
        "selected": draw_selected(jax.random.fold_in(jax.random.fold_in(arg_keys[6], part), 71), part),
    }


score_scale = 192.0 ** -0.5
floor_value = -1.0e30


def attend_query(latent_cache, query_rows, chosen):
    key_rows = jnp.take(latent_cache, chosen, axis=0).astype(jnp.float32)
    scores = jnp.einsum("hd,kd->hk", query_rows.astype(jnp.float32), key_rows) * score_scale
    highest = jnp.max(scores, axis=1, keepdims=True)
    expo = jnp.exp(scores - highest)
    total = jnp.sum(expo, axis=1, keepdims=True)
    rounded = lax.optimization_barrier(expo.astype(jnp.bfloat16))
    weights = rounded.astype(jnp.float32)
    mixed = jnp.einsum("hk,kd->hd", weights, key_rows[:, :LATENT])
    return (mixed / total).astype(jnp.bfloat16)


def masked_lse(scores, keep_mask):
    highest = jnp.max(jnp.where(keep_mask, scores, floor_value), axis=1)
    summed = jnp.sum(jnp.where(keep_mask, jnp.exp(scores - highest[:, None]), 0.0), axis=1)
    return highest + jnp.log(summed)


def index_block(query_rows, weight_rows, chosen, positions, index_keys):
    row_count = query_rows.shape[0]
    stacked = query_rows.reshape(row_count * IHEADS, IWIDTH)
    products = jnp.dot(stacked, index_keys.T, preferred_element_type=jnp.float32)
    rectified = jnp.maximum(products, 0.0).reshape(row_count, IHEADS, KEYS)
    index_scale = float(IHEADS * IWIDTH) ** -0.5
    scores = jnp.sum(weight_rows[:, :, None] * rectified, axis=1) * index_scale
    key_places = jnp.arange(KEYS).astype(jnp.int32)
    causal = key_places[None, :] <= positions[:, None]
    all_lse = masked_lse(scores, causal)
    picked = jnp.take_along_axis(scores, chosen, axis=1)
    sel_highest = jnp.max(picked, axis=1)
    sel_lse = sel_highest + jnp.log(jnp.sum(jnp.exp(picked - sel_highest[:, None]), axis=1))
    return sel_lse - all_lse


def reference(att_query, latent_cache, index_query, index_weight, index_keys, selected):
    selections = selected.reshape(QUERIES, TOPK)
    queries = att_query.reshape(QUERIES, HEADS, LATENT + ROPE)
    attended = lax.map(lambda paired: attend_query(latent_cache, paired[0], paired[1]), (queries, selections))
    positions = (KEYS - QUERIES + jnp.arange(QUERIES)).astype(jnp.int32)
    groups_count = QUERIES // 8
    shares = lax.map(
        lambda grouped: index_block(grouped[0], grouped[1], grouped[2], grouped[3], index_keys),
        (index_query.reshape(groups_count, 8, IHEADS * IWIDTH),
         index_weight.reshape(groups_count, 8, IHEADS),
         selections.reshape(groups_count, 8, TOPK),
         positions.reshape(groups_count, 8)))
    return attended.reshape(QBLOCKS, QB, HEADS * LATENT), shares.reshape(QBLOCKS, QB)
```

```python
import functools

import jax
import jax.numpy as jnp
from jax import lax
from jax.experimental import pallas as pl
from jax.experimental.pallas import tpu as pltpu
from jax.sharding import PartitionSpec as P

HEADS = 64
LATENT = 512
CHUNKS = 2
PIECES = 3
RELAY_X = 2
TILE = 16
LANES = 128

score_scale = 192.0 ** (-0.5)
floor_value = -1e30
MESH = pl.DeviceIdType.MESH


def dot_nt(a, b):
    return lax.dot_general(a, b, (((1,), (1,)), ((), ())), preferred_element_type=jnp.float32)


def kernel(
    n,
    pb_total,
    q_ref,
    latent_ref,
    iq_ref,
    iw_ref,
    ik_ref,
    sel_ref,
    out_ref,
    share_ref,
    kv_a,
    kv_b,
    row_send,
    row_recv,
    share_send,
    share_recv,
    mask_ref,
    m_ref,
    l_ref,
    acc_ref,
    q_rows,
    out_rows,
    q_both,
    part_send,
    part_recv,
    stat_send,
    stat_recv,
    own_sem,
    ring_send,
    ring_recv,
    pair_send,
    pair_recv,
    row_ssem,
    row_rsem,
    share_ssem,
    share_rsem,
    twin_ssem,
    twin_rsem,
    entered,
):
    ring = n // 2
    half = ring // 2
    row_width, keys_here = latent_ref.shape
    per_block = iq_ref.shape[0]
    top_count = sel_ref.shape[1]
    head_count = iw_ref.shape[1]
    width = ik_ref.shape[1]
    part = row_width // 2
    cuts = [TILE * (k * (part // TILE) // CHUNKS) for k in range(CHUNKS)] + [part]

    me = lax.axis_index("ctx")
    pb = lax.axis_index("pb")
    core = lax.rem(pb, 2)
    partner = pb + 1 - 2 * core

    first = (me // ring) * ring
    twin = lax.rem(me + ring, n)
    spot = me - first
    place = jnp.where(lax.rem(spot, 2) == 0, spot // 2, ring - 1 - spot // 2)
    turn = 1 - 2 * core

    def along(steps):
        at = lax.rem(place + turn * steps + 2 * ring, ring)
        return first + jnp.where(at < half, 2 * at, 2 * (ring - 1 - at) + 1)

    next_a = along(1)
    next_b = along(-1)

    barrier = pltpu.get_barrier_semaphore()
    for peer in (next_a, next_b, twin):
        pl.semaphore_signal(barrier, inc=1, device_id={"ctx": peer}, device_id_type=MESH)
    pl.semaphore_signal(barrier, inc=1, device_id={"pb": partner}, device_id_type=MESH)

    own_copy = pltpu.make_async_copy(latent_ref, kv_a.at[0], own_sem)
    own_copy.start()

    sel = sel_ref[...]
    starts = lax.broadcasted_iota(jnp.int32, (n, top_count), 0) * keys_here
    in_block = (sel >= starts) & (sel < starts + keys_here)
    base = jnp.sum(jnp.where(in_block, starts, 0), axis=0, keepdims=True)
    local = sel - base
    lanes = lax.broadcasted_iota(jnp.int32, (keys_here, top_count), 0)
    mask = dot_nt(
        in_block.astype(jnp.float32).astype(jnp.bfloat16),
        (local == lanes).astype(jnp.float32).astype(jnp.bfloat16),
    )
    for d in range(n):
        mask_ref[0, d] = mask[d : d + 1]

    pairs = HEADS // 2
    groups = 2 * row_width // LANES
    q_rows[...] = q_ref[0].astype(jnp.float32).reshape(pairs * groups, LANES)
    joined = jnp.concatenate(
        [q_rows[pl.ds(g, pairs, stride=groups), :] for g in range(groups)], axis=1
    )
    q_both[0] = jnp.concatenate(
        [joined[:, :row_width], joined[:, row_width:]], axis=0
    ).astype(jnp.bfloat16)

    wide = iq_ref[...].astype(jnp.float32)
    stacked = jnp.concatenate(
        [wide[:, j * width : (j + 1) * width] for j in range(head_count)], axis=0
    ).astype(jnp.bfloat16)
    products = dot_nt(stacked, ik_ref[...])
    weights = iw_ref[...]
    index = jnp.zeros((per_block, keys_here), jnp.float32)
    for j in range(head_count):
        index += weights[:, j : j + 1] * jnp.maximum(
            products[j * per_block : (j + 1) * per_block], 0.0
        )
    index = index * (float(head_count * width) ** (-0.5))
    for r in range(per_block):
        row_send[r] = index[r : r + 1]
    row_recv[me] = row_send[me]

    pl.semaphore_wait(barrier, 4)

    def piece(k, of=core):
        return pl.ds(pl.multiple_of(of * part + cuts[k], TILE), cuts[k + 1] - cuts[k])

    def hop_a(s, k):
        source = latent_ref if s == 1 else kv_a.at[s - 1]
        return pltpu.make_async_remote_copy(
            src_ref=source.at[piece(k)],
            dst_ref=kv_a.at[s, piece(k)],
            send_sem=ring_send.at[0, s, k],
            recv_sem=ring_recv.at[0, s, k],
            device_id={"ctx": next_a},
            device_id_type=MESH,
        )

    def hop_b(s, k):
        source = latent_ref if s == 1 else kv_b.at[s - 1]
        return pltpu.make_async_remote_copy(
            src_ref=source.at[piece(k)],
            dst_ref=kv_b.at[s, piece(k)],
            send_sem=ring_send.at[1, s, k],
            recv_sem=ring_recv.at[1, s, k],
            device_id={"ctx": next_b},
            device_id_type=MESH,
        )

    def swap(side, s, k):
        source = (kv_a if side == 0 else kv_b).at[s, piece(k)]
        to_a = side == 1 or s == half
        target = (kv_a if to_a else kv_b).at[s, piece(k)]
        return pltpu.make_async_remote_copy(
            src_ref=source,
            dst_ref=target,
            send_sem=pair_send.at[side, s, k],
            recv_sem=pair_recv.at[0 if to_a else 1, s, k],
            device_id={"pb": partner},
            device_id_type=MESH,
        )

    def swap_wait(side, s, k):
        target = (kv_a if side == 0 else kv_b).at[s, piece(k, 1 - core)]
        pltpu.make_async_remote_copy(
            src_ref=target,
            dst_ref=target,
            send_sem=pair_send.at[side, s, k],
            recv_sem=pair_recv.at[side, s, k],
            device_id={"pb": partner},
            device_id_type=MESH,
        ).wait_recv()

    def row_copy(o):
        to = lax.rem(me + o, n)
        return pltpu.make_async_remote_copy(
            src_ref=row_send.at[to],
            dst_ref=row_recv.at[me],
            send_sem=row_ssem.at[o],
            recv_sem=row_rsem.at[o],
            device_id={"ctx": to},
            device_id_type=MESH,
        )

    def share_copy(o):
        to = lax.rem(me + o, n)
        return pltpu.make_async_remote_copy(
            src_ref=share_send,
            dst_ref=share_recv.at[me],
            send_sem=share_ssem.at[o],
            recv_sem=share_rsem.at[o],
            device_id={"ctx": to},
            device_id_type=MESH,
        )

    def to_twin(j):
        source, target = (
            (mask_ref.at[0], mask_ref.at[1]),
            (q_both.at[0], q_both.at[1]),
            (stat_send, stat_recv),
            (part_send, part_recv),
        )[j]
        return pltpu.make_async_remote_copy(
            src_ref=source,
            dst_ref=target,
            send_sem=twin_ssem.at[j],
            recv_sem=twin_rsem.at[j],
            device_id={"ctx": twin},
            device_id_type=MESH,
        )

    for k in range(CHUNKS):
        hop_a(1, k).start()
        if half > 1:
            hop_b(1, k).start()
    to_twin(0).start()
    to_twin(1).start()

    for r in range(half):
        for peer in (next_a, next_b, twin):
            pl.semaphore_signal(
                entered.at[r], inc=1, device_id={"ctx": peer}, device_id_type=MESH
            )
        pl.semaphore_wait(entered.at[r], 3)
    for o in range(1, n):
        row_copy(o).start()

    def attend(which, blocks, fresh=False):
        pieces = []
        for slot, owner in blocks:
            s = jnp.dot(q_both[which], slot[...], preferred_element_type=jnp.float32) * score_scale
            pieces.append(jnp.where(mask_ref[which, owner] > 0.5, s, floor_value))
        peak = functools.reduce(
            jnp.maximum, [jnp.max(s, axis=1, keepdims=True) for s in pieces]
        )
        if not fresh:
            before = m_ref[which]
            peak = jnp.maximum(before, peak)
            fade = jnp.exp(before - peak)
        total = None
        mixed = None
        for s, (slot, owner) in zip(pieces, blocks):
            expo = jnp.exp(s - peak)
            summed = jnp.sum(expo, axis=1, keepdims=True)
            product = dot_nt(expo.astype(jnp.bfloat16), slot[:LATENT, :])
            total = summed if total is None else total + summed
            mixed = product if mixed is None else mixed + product
        if not fresh:
            total = total + fade * l_ref[which]
            mixed = mixed + fade * acc_ref[which]
        return peak, total, mixed

    def attend_store(which, blocks, fresh=False):
        peak, total, mixed = attend(which, blocks, fresh)
        m_ref[which] = peak
        l_ref[which] = total
        acc_ref[which] = mixed

    own_copy.wait()
    attend_store(0, [(kv_a.at[0], me)], True)

    def share_here():
        for o in range(1, n):
            row_copy(o).wait_recv()
        scores = jnp.concatenate([row_recv[d] for d in range(n)], axis=0)
        places = lax.broadcasted_iota(jnp.int32, (n, keys_here), 0) * keys_here
        places = places + lax.broadcasted_iota(jnp.int32, (n, keys_here), 1)
        mine = n * keys_here - pb_total * per_block + pb * per_block + me

        def lse(keep):
            kept = jnp.where(keep, scores, floor_value)
            top = jnp.max(jnp.max(kept, axis=1, keepdims=True), axis=0, keepdims=True)
            terms = jnp.where(keep, jnp.exp(kept - top), 0.0)
            summed = jnp.sum(jnp.sum(terms, axis=1, keepdims=True), axis=0, keepdims=True)
            return top + jnp.log(summed)

        share = lse(mask > 0.5) - lse(places <= mine)
        share_send[...] = jnp.broadcast_to(share, share_send.shape)
        share_recv[me] = share_send[...]

    for s in range(1, half + 1):
        for k in range(CHUNKS):
            hop_a(s, k).wait_recv()
            if s < half:
                hop_a(s + 1, k).start()
            swap(0, s, k).start()
            if s < half:
                hop_b(s, k).wait_recv()
                if s + 1 < half:
                    hop_b(s + 1, k).start()
                swap(1, s, k).start()
        if s == 1:
            to_twin(0).wait_recv()
            to_twin(1).wait_recv()
            attend_store(1, [(kv_a.at[0], me)], True)
        if s == 1:
            share_here()
        if s == min(2, half):
            for o in range(1, n):
                share_copy(o).start()
        if s > 1:
            for k in range(CHUNKS):
                swap_wait(0, s - 1, k)
                swap_wait(1, s - 1, k)
            near = [(kv_a.at[s - 1], along(1 - s)), (kv_b.at[s - 1], along(s - 1))]
            attend_store(1, near)
            if s < half:
                attend_store(0, near)

    for k in range(CHUNKS):
        swap_wait(0, half, k)
    last = [(kv_a.at[half], along(half))]
    square = (HEADS, HEADS)
    eye = lax.broadcasted_iota(jnp.int32, square, 0) == lax.broadcasted_iota(jnp.int32, square, 1)

    def as_row(column):
        return jnp.sum(jnp.where(eye, column, 0.0), axis=0, keepdims=True)

    def as_column(row):
        return jnp.sum(jnp.where(eye, row, 0.0), axis=1, keepdims=True)

    peak, total, mixed = attend(1, last)
    part_send[...] = (mixed / total).astype(jnp.bfloat16)
    stat_send[...] = jnp.concatenate([as_row(peak), as_row(total)], axis=0)
    to_twin(3).start()
    to_twin(2).start()
    peak, total, mixed = attend(0, near + last)
    to_twin(2).wait_recv()
    to_twin(3).wait_recv()
    other_peak = as_column(stat_recv[0:1])
    other_total = as_column(stat_recv[1:2])
    top = jnp.maximum(peak, other_peak)
    scale = jnp.exp(peak - top)
    other = jnp.exp(other_peak - top) * other_total
    mixed = scale * mixed + other * part_recv[...].astype(jnp.float32)
    result = mixed / (scale * total + other)
    spans = LATENT // LANES
    for side in range(2):
        for g in range(spans):
            out_rows[pl.ds(side * spans + g, pairs, stride=2 * spans), :] = result[
                side * pairs : (side + 1) * pairs, g * LANES : (g + 1) * LANES
            ]
    out_ref[...] = out_rows[...].astype(jnp.bfloat16)

    for o in range(1, n):
        share_copy(o).wait_recv()
    spots = lax.broadcasted_iota(jnp.int32, share_ref.shape, 1)
    shares = jnp.zeros(share_ref.shape, jnp.float32)
    for d in range(n):
        shares = jnp.where(spots == d, share_recv[d][:, : share_ref.shape[1]], shares)
    share_ref[...] = shares

    for o in range(1, n):
        row_copy(o).wait_send()
        share_copy(o).wait_send()
    for j in range(4):
        to_twin(j).wait_send()
    for s in range(1, half + 1):
        for k in range(CHUNKS):
            hop_a(s, k).wait_send()
            swap(0, s, k).wait_send()
            if s < half:
                hop_b(s, k).wait_send()
                swap(1, s, k).wait_send()


def square_kernel(
    n,
    pb_total,
    q_hbm,
    latent_hbm,
    iq_hbm,
    iw_hbm,
    ik_hbm,
    sel_hbm,
    out_ref,
    share_ref,
    q_in,
    iq_ref,
    iw_ref,
    ik_ref,
    sel_ref,
    kv,
    row_send,
    row_recv,
    share_send,
    share_recv,
    mask_ref,
    m_ref,
    l_ref,
    acc_ref,
    q_rows,
    q_both,
    part_send,
    part_recv,
    stat_send,
    stat_recv,
    load_sem,
    own_ssem,
    relay_ssem,
    kv_rsem,
    swap_ssem,
    swap_rsem,
    row_ssem,
    row_rsem,
    share_ssem,
    share_rsem,
    twin_ssem,
    twin_rsem,
    entered,
):
    ring = n // 2
    row_width, keys_here = latent_hbm.shape
    per_block = iq_ref.shape[0]
    top_count = sel_ref.shape[1]
    head_count = iw_ref.shape[1]
    width = ik_ref.shape[1]
    part = row_width // 2
    cuts = [TILE * (k * (part // TILE) // PIECES) for k in range(PIECES)] + [part]

    me = lax.axis_index("ctx")
    pb = lax.axis_index("pb")
    core = lax.rem(pb, 2)
    partner = pb + 1 - 2 * core

    first = (me // ring) * ring
    twin = lax.rem(me + ring, n)
    twin_first = lax.rem(first + ring, n)
    spot = me - first
    side = lax.rem(spot, 2)
    mate_x = first + spot + 1 - 2 * side
    mate_z = first + lax.rem(spot + 2, ring)
    diagonal = first + ring - 1 - spot

    barrier = pltpu.get_barrier_semaphore()
    for peer in (twin, diagonal, mate_z, mate_x):
        pl.semaphore_signal(barrier, inc=1, device_id={"ctx": peer}, device_id_type=MESH)
    pl.semaphore_signal(barrier, inc=1, device_id={"pb": partner}, device_id_type=MESH)

    def load(j):
        source, target = (
            (q_hbm, q_in),
            (sel_hbm, sel_ref),
            (iq_hbm, iq_ref),
            (ik_hbm, ik_ref),
            (iw_hbm, iw_ref),
            (latent_hbm, kv.at[0]),
        )[j]
        return pltpu.make_async_copy(source, target, load_sem.at[j])

    for j in range(6):
        load(j).start()

    pairs = HEADS // 2
    groups = 2 * row_width // LANES
    load(0).wait()
    q_rows[...] = q_in[0].astype(jnp.float32).reshape(pairs * groups, LANES)
    joined = jnp.concatenate(
        [q_rows[pl.ds(g, pairs, stride=groups), :] for g in range(groups)], axis=1
    )
    q_both[0] = jnp.concatenate(
        [joined[:, :row_width], joined[:, row_width:]], axis=0
    ).astype(jnp.bfloat16)

    load(1).wait()
    sel = sel_ref[...]
    starts = lax.broadcasted_iota(jnp.int32, (n, top_count), 0) * keys_here
    in_block = (sel >= starts) & (sel < starts + keys_here)
    base = jnp.sum(jnp.where(in_block, starts, 0), axis=0, keepdims=True)
    local = sel - base
    lanes = lax.broadcasted_iota(jnp.int32, (keys_here, top_count), 0)
    mask = dot_nt(
        in_block.astype(jnp.float32).astype(jnp.bfloat16),
        (local == lanes).astype(jnp.float32).astype(jnp.bfloat16),
    )
    for d in range(n):
        mask_ref[0, d] = mask[d : d + 1]

    def piece(k, of=core):
        return pl.ds(pl.multiple_of(of * part + cuts[k], TILE), cuts[k + 1] - cuts[k])

    def remote(source, target, send_sem, recv_sem, **device):
        return pltpu.make_async_remote_copy(
            src_ref=source,
            dst_ref=target,
            send_sem=send_sem,
            recv_sem=recv_sem,
            device_id=device,
            device_id_type=MESH,
        )

    def own(axis, k):
        return remote(
            latent_hbm.at[piece(k)],
            kv.at[1 + axis, piece(k)],
            own_ssem.at[axis, k],
            kv_rsem.at[axis, k],
            ctx=(mate_x, mate_z)[axis],
        )

    def relay(k):
        by_x = k < RELAY_X
        return remote(
            kv.at[2 if by_x else 1, piece(k)],
            kv.at[3, piece(k)],
            relay_ssem.at[k],
            kv_rsem.at[2, k],
            ctx=mate_x if by_x else mate_z,
        )

    def swap(slot, k, of=core):
        return remote(
            kv.at[slot, piece(k, of)],
            kv.at[slot, piece(k, of)],
            swap_ssem.at[slot - 1, k],
            swap_rsem.at[slot - 1, k],
            pb=partner,
        )

    def swap_wait(slot):
        for k in range(PIECES):
            swap(slot, k, 1 - core).wait_recv()

    def row_copy(o):
        to = lax.rem(me + o, n)
        return remote(
            row_send.at[to], row_recv.at[me], row_ssem.at[o], row_rsem.at[o], ctx=to
        )

    def share_copy(o):
        to = lax.rem(me + o, n)
        return remote(
            share_send, share_recv.at[me], share_ssem.at[o], share_rsem.at[o], ctx=to
        )

    def to_twin(j):
        there = pl.ds(twin_first, ring)
        source, target = (
            (mask_ref.at[0, there], mask_ref.at[1, there]),
            (q_both.at[0], q_both.at[1]),
            (stat_send, stat_recv),
            (part_send, part_recv),
        )[j]
        return remote(source, target, twin_ssem.at[j], twin_rsem.at[j], ctx=twin)

    pl.semaphore_wait(barrier, 5)

    by_x = list(range(RELAY_X))
    by_z = list(range(RELAY_X, PIECES))
    x_order = by_z + by_x
    z_order = by_x + by_z
    for i in range(PIECES):
        if i == RELAY_X:
            to_twin(0).start()
            to_twin(1).start()
        own(0, x_order[i]).start()
        own(1, z_order[i]).start()

    pl.semaphore_signal(entered, inc=1, device_id={"ctx": twin}, device_id_type=MESH)

    for j in (2, 3, 4):
        load(j).wait()
    wide = iq_ref[...].astype(jnp.float32)
    stacked = jnp.concatenate(
        [wide[:, j * width : (j + 1) * width] for j in range(head_count)], axis=0
    ).astype(jnp.bfloat16)
    products = dot_nt(stacked, ik_ref[...])
    weights = iw_ref[...]
    index = jnp.zeros((per_block, keys_here), jnp.float32)
    for j in range(head_count):
        index += weights[:, j : j + 1] * jnp.maximum(
            products[j * per_block : (j + 1) * per_block], 0.0
        )
    index = index * (float(head_count * width) ** (-0.5))
    for r in range(per_block):
        row_send[r] = index[r : r + 1]
    row_recv[me] = row_send[me]

    pl.semaphore_wait(entered, 1)
    for o in range(1, n):
        row_copy(o).start()

    def attend(which, blocks, fresh=False):
        pieces = []
        for slot, owner in blocks:
            s = jnp.dot(q_both[which], kv[slot], preferred_element_type=jnp.float32) * score_scale
            pieces.append(jnp.where(mask_ref[which, owner] > 0.5, s, floor_value))
        peak = functools.reduce(
            jnp.maximum, [jnp.max(s, axis=1, keepdims=True) for s in pieces]
        )
        if not fresh:
            before = m_ref[which]
            peak = jnp.maximum(before, peak)
            fade = jnp.exp(before - peak)
        total = None
        mixed = None
        for s, (slot, owner) in zip(pieces, blocks):
            expo = jnp.exp(s - peak)
            summed = jnp.sum(expo, axis=1, keepdims=True)
            product = dot_nt(expo.astype(jnp.bfloat16), kv[slot, :LATENT, :])
            total = summed if total is None else total + summed
            mixed = product if mixed is None else mixed + product
        if not fresh:
            total = total + fade * l_ref[which]
            mixed = mixed + fade * acc_ref[which]
        return peak, total, mixed

    def attend_store(which, blocks, fresh=False):
        peak, total, mixed = attend(which, blocks, fresh)
        m_ref[which] = peak
        l_ref[which] = total
        acc_ref[which] = mixed

    here = [(0, me)]
    near = [(1, mate_x), (2, mate_z)]
    last = [(3, diagonal)]

    load(5).wait()
    attend_store(0, here, True)

    for i in range(PIECES):
        for axis, k in ((0, x_order[i]), (1, z_order[i])):
            own(axis, k).wait_recv()
            if (axis == 1) == (k < RELAY_X):
                relay(k).start()
            swap(1 + axis, k).start()

    to_twin(0).wait_recv()
    to_twin(1).wait_recv()
    attend_store(1, here, True)
    swap_wait(1)
    swap_wait(2)
    attend_store(1, near)
    for k in range(PIECES):
        relay(k).wait_recv()
        swap(3, k).start()
    attend_store(0, near)

    for o in range(1, n):
        row_copy(o).wait_recv()
    scores = jnp.concatenate([row_recv[d] for d in range(n)], axis=0)
    places = lax.broadcasted_iota(jnp.int32, (n, keys_here), 0) * keys_here
    places = places + lax.broadcasted_iota(jnp.int32, (n, keys_here), 1)
    mine = n * keys_here - pb_total * per_block + pb * per_block + me

    def lse(keep):
        kept = jnp.where(keep, scores, floor_value)
        top = jnp.max(jnp.max(kept, axis=1, keepdims=True), axis=0, keepdims=True)
        terms = jnp.where(keep, jnp.exp(kept - top), 0.0)
        summed = jnp.sum(jnp.sum(terms, axis=1, keepdims=True), axis=0, keepdims=True)
        return top + jnp.log(summed)

    share = lse(mask > 0.5) - lse(places <= mine)
    share_send[...] = jnp.broadcast_to(share, share_send.shape)
    share_recv[me] = share_send[...]
    for o in range(1, n):
        share_copy(o).start()

    square = (HEADS, HEADS)
    eye = lax.broadcasted_iota(jnp.int32, square, 0) == lax.broadcasted_iota(jnp.int32, square, 1)

    def as_row(column):
        return jnp.sum(jnp.where(eye, column, 0.0), axis=0, keepdims=True)

    def as_column(row):
        return jnp.sum(jnp.where(eye, row, 0.0), axis=1, keepdims=True)

    swap_wait(3)
    peak, total, mixed = attend(1, last)
    part_send[...] = (mixed / total).astype(jnp.bfloat16)
    to_twin(3).start()
    stat_send[...] = jnp.concatenate([as_row(peak), as_row(total)], axis=0)
    to_twin(2).start()
    peak, total, mixed = attend(0, last)
    to_twin(2).wait_recv()
    other_peak = as_column(stat_recv[0:1])
    other_total = as_column(stat_recv[1:2])
    top = jnp.maximum(peak, other_peak)
    scale = jnp.exp(peak - top)
    other = jnp.exp(other_peak - top) * other_total
    whole = scale * total + other
    mixed = mixed * (scale / whole)
    other = other / whole
    to_twin(3).wait_recv()
    result = mixed + other * part_recv[...].astype(jnp.float32)
    spans = LATENT // LANES
    for odd in range(2):
        for g in range(spans):
            out_ref[pl.ds(odd * spans + g, pairs, stride=2 * spans), :] = result[
                odd * pairs : (odd + 1) * pairs, g * LANES : (g + 1) * LANES
            ]

    for o in range(1, n):
        share_copy(o).wait_recv()
    spots = lax.broadcasted_iota(jnp.int32, share_ref.shape, 1)
    shares = jnp.zeros(share_ref.shape, jnp.float32)
    for d in range(n):
        shares = jnp.where(spots == d, share_recv[d][:, : share_ref.shape[1]], shares)
    share_ref[...] = shares

    for o in range(1, n):
        row_copy(o).wait_send()
        share_copy(o).wait_send()
    for j in range(4):
        to_twin(j).wait_send()
    for k in range(PIECES):
        own(0, k).wait_send()
        own(1, k).wait_send()
        relay(k).wait_send()
        for slot in (1, 2, 3):
            swap(slot, k).wait_send()


def square_call(n, pb_total, operands):
    att_query, latent, index_query, index_weight, index_keys, selected = operands
    row_width, keys_here = latent.shape
    per_block = index_query.shape[0]
    vmem = pl.BlockSpec(memory_space=pltpu.VMEM)
    dma = pltpu.SemaphoreType.DMA
    return pl.pallas_call(
        functools.partial(square_kernel, n, pb_total),
        out_shape=(
            pltpu.VMEM((HEADS * LATENT // LANES, LANES), jnp.float32),
            pltpu.VMEM((1, per_block), jnp.float32),
        ),
        in_specs=[pl.BlockSpec(memory_space=pl.ANY)] * 6,
        out_specs=(vmem, vmem),
        scratch_shapes=[
            pltpu.VMEM(att_query.shape, att_query.dtype),
            pltpu.VMEM(index_query.shape, index_query.dtype),
            pltpu.VMEM(index_weight.shape, index_weight.dtype),
            pltpu.VMEM(index_keys.shape, index_keys.dtype),
            pltpu.VMEM(selected.shape, selected.dtype),
            pltpu.VMEM((n // 2, row_width, keys_here), jnp.bfloat16),
            pltpu.VMEM((per_block, 1, keys_here), jnp.float32),
            pltpu.VMEM((n, 1, keys_here), jnp.float32),
            pltpu.VMEM((1, LANES), jnp.float32),
            pltpu.VMEM((n, 1, LANES), jnp.float32),
            pltpu.VMEM((2, n, 1, keys_here), jnp.float32),
            pltpu.VMEM((2, HEADS, 1), jnp.float32),
            pltpu.VMEM((2, HEADS, 1), jnp.float32),
            pltpu.VMEM((2, HEADS, LATENT), jnp.float32),
            pltpu.VMEM((HEADS * row_width // LANES, LANES), jnp.float32),
            pltpu.VMEM((2, HEADS, row_width), jnp.bfloat16),
            pltpu.VMEM((HEADS, LATENT), jnp.bfloat16),
            pltpu.VMEM((HEADS, LATENT), jnp.bfloat16),
            pltpu.VMEM((2, HEADS), jnp.float32),
            pltpu.VMEM((2, HEADS), jnp.float32),
            dma((6,)),
            dma((2, PIECES)),
            dma((PIECES,)),
            dma((3, PIECES)),
            dma((3, PIECES)),
            dma((3, PIECES)),
            dma((n,)),
            dma((n,)),
            dma((n,)),
            dma((n,)),
            dma((4,)),
            dma((4,)),
            pltpu.SemaphoreType.REGULAR,
        ],
        compiler_params=pltpu.CompilerParams(collective_id=0, has_side_effects=True),
        name="sparse_prefill",
    )(*operands)


def ring_call(n, pb_total, operands):
    half = n // 4
    latent, per_block = operands[1], operands[2].shape[0]
    row_width, keys_here = latent.shape
    vmem = pl.BlockSpec(memory_space=pltpu.VMEM)
    dma = pltpu.SemaphoreType.DMA
    return pl.pallas_call(
        functools.partial(kernel, n, pb_total),
        out_shape=(
            pltpu.VMEM((HEADS * LATENT // LANES, LANES), jnp.bfloat16),
            pltpu.VMEM((1, per_block), jnp.float32),
        ),
        in_specs=[vmem, pl.BlockSpec(memory_space=pl.ANY), vmem, vmem, vmem, vmem],
        out_specs=(vmem, vmem),
        scratch_shapes=[
            pltpu.VMEM((half + 1, row_width, keys_here), jnp.bfloat16),
            pltpu.VMEM((half, row_width, keys_here), jnp.bfloat16),
            pltpu.VMEM((per_block, 1, keys_here), jnp.float32),
            pltpu.VMEM((n, 1, keys_here), jnp.float32),
            pltpu.VMEM((1, 128), jnp.float32),
            pltpu.VMEM((n, 1, 128), jnp.float32),
            pltpu.VMEM((2, n, 1, keys_here), jnp.float32),
            pltpu.VMEM((2, HEADS, 1), jnp.float32),
            pltpu.VMEM((2, HEADS, 1), jnp.float32),
            pltpu.VMEM((2, HEADS, LATENT), jnp.float32),
            pltpu.VMEM((HEADS * row_width // LANES, LANES), jnp.float32),
            pltpu.VMEM((HEADS * LATENT // LANES, LANES), jnp.float32),
            pltpu.VMEM((2, HEADS, row_width), jnp.bfloat16),
            pltpu.VMEM((HEADS, LATENT), jnp.bfloat16),
            pltpu.VMEM((HEADS, LATENT), jnp.bfloat16),
            pltpu.VMEM((2, HEADS), jnp.float32),
            pltpu.VMEM((2, HEADS), jnp.float32),
            dma,
            dma((2, half + 1, CHUNKS)),
            dma((2, half + 1, CHUNKS)),
            dma((2, half + 1, CHUNKS)),
            dma((2, half + 1, CHUNKS)),
            dma((n,)),
            dma((n,)),
            dma((n,)),
            dma((n,)),
            dma((4,)),
            dma((4,)),
            pltpu.SemaphoreType.REGULAR((half,)),
        ],
        compiler_params=pltpu.CompilerParams(collective_id=0, has_side_effects=True),
        name="sparse_prefill",
    )(*operands)


def finish(rows_ref, shares_ref, out_ref, share_ref):
    flat = rows_ref[...].astype(jnp.float32).reshape(1, HEADS * LATENT)
    out_ref[0] = flat.astype(jnp.bfloat16)
    share_ref[...] = shares_ref[...]


def body(n, pb_total, att_query, latent_cache, index_query, index_weight, index_keys, selected):
    per_block = index_query.shape[1]
    operands = (
        att_query,
        latent_cache.T,
        index_query[0],
        index_weight[0],
        index_keys,
        selected[0],
    )
    call = square_call if n == 8 else ring_call
    results = [
        pltpu.with_memory_space_constraint(r, pltpu.VMEM) for r in call(n, pb_total, operands)
    ]
    vmem = pl.BlockSpec(memory_space=pltpu.VMEM)
    return pl.pallas_call(
        finish,
        out_shape=(
            jax.ShapeDtypeStruct((1, 1, HEADS * LATENT), jnp.bfloat16),
            jax.ShapeDtypeStruct((1, per_block), jnp.float32),
        ),
        in_specs=[vmem, vmem],
        out_specs=(vmem, vmem),
        name="finish",
    )(*results)


def solution(mesh):
    return jax.shard_map(
        functools.partial(body, mesh.shape["ctx"], mesh.shape["pb"]),
        mesh=mesh,
        in_specs=(
            P(("groups", "pb"), "ctx", None),
            P(("groups", "ctx"), None),
            P(("groups", "pb"), None, None),
            P(("groups", "pb"), None, None),
            P(("groups", "ctx"), None),
            P(("groups", "pb"), "ctx", None),
        ),
        out_specs=(P(("groups", "pb"), "ctx", None), P(("groups", "pb"), None)),
        check_vma=False,
    )
```

```python
import functools

import jax
import jax.numpy as jnp
from jax import lax
from jax.experimental import pallas as pl
from jax.experimental.pallas import tpu as pltpu
from jax.sharding import PartitionSpec as P

HEADS = 64
LATENT = 512
CHUNKS = 2
PIECES = 4
RELAY_X = 2
TILE = 16
LANES = 128

score_scale = 192.0 ** (-0.5)
floor_value = -1e30
MESH = pl.DeviceIdType.MESH


def dot_nt(a, b):
    return lax.dot_general(a, b, (((1,), (1,)), ((), ())), preferred_element_type=jnp.float32)


def kernel(
    n,
    pb_total,
    q_ref,
    latent_ref,
    iq_ref,
    iw_ref,
    ik_ref,
    sel_ref,
    out_ref,
    share_ref,
    kv_a,
    kv_b,
    row_send,
    row_recv,
    share_send,
    share_recv,
    mask_ref,
    m_ref,
    l_ref,
    acc_ref,
    q_rows,
    out_rows,
    q_both,
    part_send,
    part_recv,
    stat_send,
    stat_recv,
    own_sem,
    ring_send,
    ring_recv,
    pair_send,
    pair_recv,
    row_ssem,
    row_rsem,
    share_ssem,
    share_rsem,
    twin_ssem,
    twin_rsem,
    entered,
):
    ring = n // 2
    half = ring // 2
    row_width, keys_here = latent_ref.shape
    per_block = iq_ref.shape[0]
    top_count = sel_ref.shape[1]
    head_count = iw_ref.shape[1]
    width = ik_ref.shape[1]
    part = row_width // 2
    cuts = [TILE * (k * (part // TILE) // CHUNKS) for k in range(CHUNKS)] + [part]

    me = lax.axis_index("ctx")
    pb = lax.axis_index("pb")
    core = lax.rem(pb, 2)
    partner = pb + 1 - 2 * core

    first = (me // ring) * ring
    twin = lax.rem(me + ring, n)
    spot = me - first
    place = jnp.where(lax.rem(spot, 2) == 0, spot // 2, ring - 1 - spot // 2)
    turn = 1 - 2 * core

    def along(steps):
        at = lax.rem(place + turn * steps + 2 * ring, ring)
        return first + jnp.where(at < half, 2 * at, 2 * (ring - 1 - at) + 1)

    next_a = along(1)
    next_b = along(-1)

    barrier = pltpu.get_barrier_semaphore()
    for peer in (next_a, next_b, twin):
        pl.semaphore_signal(barrier, inc=1, device_id={"ctx": peer}, device_id_type=MESH)
    pl.semaphore_signal(barrier, inc=1, device_id={"pb": partner}, device_id_type=MESH)

    own_copy = pltpu.make_async_copy(latent_ref, kv_a.at[0], own_sem)
    own_copy.start()

    sel = sel_ref[...]
    starts = lax.broadcasted_iota(jnp.int32, (n, top_count), 0) * keys_here
    in_block = (sel >= starts) & (sel < starts + keys_here)
    base = jnp.sum(jnp.where(in_block, starts, 0), axis=0, keepdims=True)
    local = sel - base
    lanes = lax.broadcasted_iota(jnp.int32, (keys_here, top_count), 0)
    mask = dot_nt(
        in_block.astype(jnp.float32).astype(jnp.bfloat16),
        (local == lanes).astype(jnp.float32).astype(jnp.bfloat16),
    )
    for d in range(n):
        mask_ref[0, d] = mask[d : d + 1]

    pairs = HEADS // 2
    groups = 2 * row_width // LANES
    q_rows[...] = q_ref[0].astype(jnp.float32).reshape(pairs * groups, LANES)
    joined = jnp.concatenate(
        [q_rows[pl.ds(g, pairs, stride=groups), :] for g in range(groups)], axis=1
    )
    q_both[0] = jnp.concatenate(
        [joined[:, :row_width], joined[:, row_width:]], axis=0
    ).astype(jnp.bfloat16)

    wide = iq_ref[...].astype(jnp.float32)
    stacked = jnp.concatenate(
        [wide[:, j * width : (j + 1) * width] for j in range(head_count)], axis=0
    ).astype(jnp.bfloat16)
    products = dot_nt(stacked, ik_ref[...])
    weights = iw_ref[...]
    index = jnp.zeros((per_block, keys_here), jnp.float32)
    for j in range(head_count):
        index += weights[:, j : j + 1] * jnp.maximum(
            products[j * per_block : (j + 1) * per_block], 0.0
        )
    index = index * (float(head_count * width) ** (-0.5))
    for r in range(per_block):
        row_send[r] = index[r : r + 1]
    row_recv[me] = row_send[me]

    pl.semaphore_wait(barrier, 4)

    def piece(k, of=core):
        return pl.ds(pl.multiple_of(of * part + cuts[k], TILE), cuts[k + 1] - cuts[k])

    def hop_a(s, k):
        source = latent_ref if s == 1 else kv_a.at[s - 1]
        return pltpu.make_async_remote_copy(
            src_ref=source.at[piece(k)],
            dst_ref=kv_a.at[s, piece(k)],
            send_sem=ring_send.at[0, s, k],
            recv_sem=ring_recv.at[0, s, k],
            device_id={"ctx": next_a},
            device_id_type=MESH,
        )

    def hop_b(s, k):
        source = latent_ref if s == 1 else kv_b.at[s - 1]
        return pltpu.make_async_remote_copy(
            src_ref=source.at[piece(k)],
            dst_ref=kv_b.at[s, piece(k)],
            send_sem=ring_send.at[1, s, k],
            recv_sem=ring_recv.at[1, s, k],
            device_id={"ctx": next_b},
            device_id_type=MESH,
        )

    def swap(side, s, k):
        source = (kv_a if side == 0 else kv_b).at[s, piece(k)]
        to_a = side == 1 or s == half
        target = (kv_a if to_a else kv_b).at[s, piece(k)]
        return pltpu.make_async_remote_copy(
            src_ref=source,
            dst_ref=target,
            send_sem=pair_send.at[side, s, k],
            recv_sem=pair_recv.at[0 if to_a else 1, s, k],
            device_id={"pb": partner},
            device_id_type=MESH,
        )

    def swap_wait(side, s, k):
        target = (kv_a if side == 0 else kv_b).at[s, piece(k, 1 - core)]
        pltpu.make_async_remote_copy(
            src_ref=target,
            dst_ref=target,
            send_sem=pair_send.at[side, s, k],
            recv_sem=pair_recv.at[side, s, k],
            device_id={"pb": partner},
            device_id_type=MESH,
        ).wait_recv()

    def row_copy(o):
        to = lax.rem(me + o, n)
        return pltpu.make_async_remote_copy(
            src_ref=row_send.at[to],
            dst_ref=row_recv.at[me],
            send_sem=row_ssem.at[o],
            recv_sem=row_rsem.at[o],
            device_id={"ctx": to},
            device_id_type=MESH,
        )

    def share_copy(o):
        to = lax.rem(me + o, n)
        return pltpu.make_async_remote_copy(
            src_ref=share_send,
            dst_ref=share_recv.at[me],
            send_sem=share_ssem.at[o],
            recv_sem=share_rsem.at[o],
            device_id={"ctx": to},
            device_id_type=MESH,
        )

    def to_twin(j):
        source, target = (
            (mask_ref.at[0], mask_ref.at[1]),
            (q_both.at[0], q_both.at[1]),
            (stat_send, stat_recv),
            (part_send, part_recv),
        )[j]
        return pltpu.make_async_remote_copy(
            src_ref=source,
            dst_ref=target,
            send_sem=twin_ssem.at[j],
            recv_sem=twin_rsem.at[j],
            device_id={"ctx": twin},
            device_id_type=MESH,
        )

    for k in range(CHUNKS):
        hop_a(1, k).start()
        if half > 1:
            hop_b(1, k).start()
    to_twin(0).start()
    to_twin(1).start()

    for r in range(half):
        for peer in (next_a, next_b, twin):
            pl.semaphore_signal(
                entered.at[r], inc=1, device_id={"ctx": peer}, device_id_type=MESH
            )
        pl.semaphore_wait(entered.at[r], 3)
    for o in range(1, n):
        row_copy(o).start()

    def attend(which, blocks, fresh=False):
        pieces = []
        for slot, owner in blocks:
            s = jnp.dot(q_both[which], slot[...], preferred_element_type=jnp.float32) * score_scale
            pieces.append(jnp.where(mask_ref[which, owner] > 0.5, s, floor_value))
        peak = functools.reduce(
            jnp.maximum, [jnp.max(s, axis=1, keepdims=True) for s in pieces]
        )
        if not fresh:
            before = m_ref[which]
            peak = jnp.maximum(before, peak)
            fade = jnp.exp(before - peak)
        total = None
        mixed = None
        for s, (slot, owner) in zip(pieces, blocks):
            expo = jnp.exp(s - peak)
            summed = jnp.sum(expo, axis=1, keepdims=True)
            product = dot_nt(expo.astype(jnp.bfloat16), slot[:LATENT, :])
            total = summed if total is None else total + summed
            mixed = product if mixed is None else mixed + product
        if not fresh:
            total = total + fade * l_ref[which]
            mixed = mixed + fade * acc_ref[which]
        return peak, total, mixed

    def attend_store(which, blocks, fresh=False):
        peak, total, mixed = attend(which, blocks, fresh)
        m_ref[which] = peak
        l_ref[which] = total
        acc_ref[which] = mixed

    own_copy.wait()
    attend_store(0, [(kv_a.at[0], me)], True)

    def share_here():
        for o in range(1, n):
            row_copy(o).wait_recv()
        scores = jnp.concatenate([row_recv[d] for d in range(n)], axis=0)
        places = lax.broadcasted_iota(jnp.int32, (n, keys_here), 0) * keys_here
        places = places + lax.broadcasted_iota(jnp.int32, (n, keys_here), 1)
        mine = n * keys_here - pb_total * per_block + pb * per_block + me

        def lse(keep):
            kept = jnp.where(keep, scores, floor_value)
            top = jnp.max(jnp.max(kept, axis=1, keepdims=True), axis=0, keepdims=True)
            terms = jnp.where(keep, jnp.exp(kept - top), 0.0)
            summed = jnp.sum(jnp.sum(terms, axis=1, keepdims=True), axis=0, keepdims=True)
            return top + jnp.log(summed)

        share = lse(mask > 0.5) - lse(places <= mine)
        share_send[...] = jnp.broadcast_to(share, share_send.shape)
        share_recv[me] = share_send[...]

    for s in range(1, half + 1):
        for k in range(CHUNKS):
            hop_a(s, k).wait_recv()
            if s < half:
                hop_a(s + 1, k).start()
            swap(0, s, k).start()
            if s < half:
                hop_b(s, k).wait_recv()
                if s + 1 < half:
                    hop_b(s + 1, k).start()
                swap(1, s, k).start()
        if s == 1:
            to_twin(0).wait_recv()
            to_twin(1).wait_recv()
            attend_store(1, [(kv_a.at[0], me)], True)
        if s == 1:
            share_here()
        if s == min(2, half):
            for o in range(1, n):
                share_copy(o).start()
        if s > 1:
            for k in range(CHUNKS):
                swap_wait(0, s - 1, k)
                swap_wait(1, s - 1, k)
            near = [(kv_a.at[s - 1], along(1 - s)), (kv_b.at[s - 1], along(s - 1))]
            attend_store(1, near)
            if s < half:
                attend_store(0, near)

    for k in range(CHUNKS):
        swap_wait(0, half, k)
    last = [(kv_a.at[half], along(half))]
    square = (HEADS, HEADS)
    eye = lax.broadcasted_iota(jnp.int32, square, 0) == lax.broadcasted_iota(jnp.int32, square, 1)

    def as_row(column):
        return jnp.sum(jnp.where(eye, column, 0.0), axis=0, keepdims=True)

    def as_column(row):
        return jnp.sum(jnp.where(eye, row, 0.0), axis=1, keepdims=True)

    peak, total, mixed = attend(1, last)
    part_send[...] = (mixed / total).astype(jnp.bfloat16)
    stat_send[...] = jnp.concatenate([as_row(peak), as_row(total)], axis=0)
    to_twin(3).start()
    to_twin(2).start()
    peak, total, mixed = attend(0, near + last)
    to_twin(2).wait_recv()
    to_twin(3).wait_recv()
    other_peak = as_column(stat_recv[0:1])
    other_total = as_column(stat_recv[1:2])
    top = jnp.maximum(peak, other_peak)
    scale = jnp.exp(peak - top)
    other = jnp.exp(other_peak - top) * other_total
    mixed = scale * mixed + other * part_recv[...].astype(jnp.float32)
    result = mixed / (scale * total + other)
    spans = LATENT // LANES
    for side in range(2):
        for g in range(spans):
            out_rows[pl.ds(side * spans + g, pairs, stride=2 * spans), :] = result[
                side * pairs : (side + 1) * pairs, g * LANES : (g + 1) * LANES
            ]
    out_ref[...] = out_rows[...].astype(jnp.bfloat16)

    for o in range(1, n):
        share_copy(o).wait_recv()
    spots = lax.broadcasted_iota(jnp.int32, share_ref.shape, 1)
    shares = jnp.zeros(share_ref.shape, jnp.float32)
    for d in range(n):
        shares = jnp.where(spots == d, share_recv[d][:, : share_ref.shape[1]], shares)
    share_ref[...] = shares

    for o in range(1, n):
        row_copy(o).wait_send()
        share_copy(o).wait_send()
    for j in range(4):
        to_twin(j).wait_send()
    for s in range(1, half + 1):
        for k in range(CHUNKS):
            hop_a(s, k).wait_send()
            swap(0, s, k).wait_send()
            if s < half:
                hop_b(s, k).wait_send()
                swap(1, s, k).wait_send()


def square_kernel(
    n,
    pb_total,
    q_hbm,
    latent_hbm,
    iq_hbm,
    iw_hbm,
    ik_hbm,
    sel_hbm,
    out_ref,
    share_ref,
    q_in,
    iq_ref,
    iw_ref,
    ik_ref,
    sel_ref,
    kv,
    row_send,
    row_recv,
    share_send,
    share_recv,
    mask_ref,
    m_ref,
    l_ref,
    acc_ref,
    q_rows,
    q_both,
    part_send,
    part_recv,
    stat_send,
    stat_recv,
    load_sem,
    own_ssem,
    relay_ssem,
    kv_rsem,
    swap_ssem,
    swap_rsem,
    row_ssem,
    row_rsem,
    share_ssem,
    share_rsem,
    twin_ssem,
    twin_rsem,
    entered,
):
    ring = n // 2
    side_count = ring // 2
    row_width, keys_here = latent_hbm.shape
    per_block = iq_ref.shape[0]
    top_count = sel_ref.shape[1]
    head_count = iw_ref.shape[1]
    width = ik_ref.shape[1]
    part = row_width // 2
    cuts = [TILE * (k * (part // TILE) // PIECES) for k in range(PIECES)] + [part]

    me = lax.axis_index("ctx")
    pb = lax.axis_index("pb")
    core = lax.rem(pb, 2)
    partner = pb + 1 - 2 * core

    first = (me // ring) * ring
    twin = lax.rem(me + ring, n)
    twin_first = lax.rem(first + ring, n)
    spot = me - first
    side = lax.rem(spot, 2)
    mate_x = first + spot + 1 - 2 * side
    mate_z = first + lax.rem(spot + 2, ring)
    diagonal = first + ring - 1 - spot
    early = me < n - side_count
    serves_early = twin < n - side_count

    barrier = pltpu.get_barrier_semaphore()
    for peer in (twin, diagonal, mate_z, mate_x):
        pl.semaphore_signal(barrier, inc=1, device_id={"ctx": peer}, device_id_type=MESH)
    pl.semaphore_signal(barrier, inc=1, device_id={"pb": partner}, device_id_type=MESH)

    def load(j):
        source, target = (
            (q_hbm, q_in),
            (sel_hbm, sel_ref),
            (iq_hbm, iq_ref),
            (ik_hbm, ik_ref),
            (iw_hbm, iw_ref),
            (latent_hbm, kv.at[0]),
        )[j]
        return pltpu.make_async_copy(source, target, load_sem.at[j])

    for j in range(6):
        load(j).start()

    pairs = HEADS // 2
    groups = 2 * row_width // LANES
    load(0).wait()
    q_rows[...] = q_in[0].astype(jnp.float32).reshape(pairs * groups, LANES)
    joined = jnp.concatenate(
        [q_rows[pl.ds(g, pairs, stride=groups), :] for g in range(groups)], axis=1
    )
    q_both[0] = jnp.concatenate(
        [joined[:, :row_width], joined[:, row_width:]], axis=0
    ).astype(jnp.bfloat16)

    def piece(k, of=core):
        return pl.ds(pl.multiple_of(of * part + cuts[k], TILE), cuts[k + 1] - cuts[k])

    def remote(source, target, send_sem, recv_sem, **device):
        return pltpu.make_async_remote_copy(
            src_ref=source,
            dst_ref=target,
            send_sem=send_sem,
            recv_sem=recv_sem,
            device_id=device,
            device_id_type=MESH,
        )

    def own(axis, k):
        return remote(
            latent_hbm.at[piece(k)],
            kv.at[1 + axis, piece(k)],
            own_ssem.at[axis, k],
            kv_rsem.at[axis, k],
            ctx=(mate_x, mate_z)[axis],
        )

    def relay(k):
        by_x = k < RELAY_X
        return remote(
            kv.at[2 if by_x else 1, piece(k)],
            kv.at[3, piece(k)],
            relay_ssem.at[k],
            kv_rsem.at[2, k],
            ctx=mate_x if by_x else mate_z,
        )

    def swap(slot, k, of=core):
        return remote(
            kv.at[slot, piece(k, of)],
            kv.at[slot, piece(k, of)],
            swap_ssem.at[slot - 1, k],
            swap_rsem.at[slot - 1, k],
            pb=partner,
        )

    def swap_wait(slot):
        for k in range(PIECES):
            swap(slot, k, 1 - core).wait_recv()

    mates = (mate_x, mate_z, diagonal)

    def row_copy(o):
        return remote(
            row_send.at[mates[o] - first],
            row_recv.at[spot],
            row_ssem.at[o],
            row_rsem.at[o],
            ctx=mates[o],
        )

    def share_copy(o):
        to = lax.rem(me + o, n)
        return remote(
            share_send, share_recv.at[me], share_ssem.at[o], share_rsem.at[o], ctx=to
        )

    def to_twin(j):
        there = pl.ds(twin_first, ring)
        source, target = (
            (mask_ref.at[0, there], mask_ref.at[1, there]),
            (q_both.at[0], q_both.at[1]),
            (stat_send, stat_recv),
            (part_send, part_recv),
        )[j]
        return remote(source, target, twin_ssem.at[j], twin_rsem.at[j], ctx=twin)

    for j in (2, 3, 4):
        load(j).wait()
    wide = iq_ref[...].astype(jnp.float32)
    stacked = jnp.concatenate(
        [wide[:, j * width : (j + 1) * width] for j in range(head_count)], axis=0
    ).astype(jnp.bfloat16)
    products = dot_nt(stacked, ik_ref[...])
    weights = iw_ref[...]
    index = jnp.zeros((per_block, keys_here), jnp.float32)
    for j in range(head_count):
        index += weights[:, j : j + 1] * jnp.maximum(
            products[j * per_block : (j + 1) * per_block], 0.0
        )
    index = index * (float(head_count * width) ** (-0.5))
    for r in range(n):
        row_send[r % ring, r // ring] = index[r : r + 1]
    row_recv[spot] = row_send[spot]

    pl.semaphore_wait(barrier, 5)

    for o in range(3):
        row_copy(o).start()

    by_x = list(range(RELAY_X))
    by_z = list(range(RELAY_X, PIECES))
    x_order = by_z + by_x
    z_order = by_x + by_z

    @pl.when(early)
    def _():
        to_twin(1).start()

    for i in range(PIECES):
        own(0, x_order[i]).start()
        own(1, z_order[i]).start()
    pl.semaphore_signal(entered, inc=1, device_id={"ctx": twin}, device_id_type=MESH)

    load(1).wait()
    sel = sel_ref[...]
    starts = lax.broadcasted_iota(jnp.int32, (n, top_count), 0) * keys_here
    in_block = (sel >= starts) & (sel < starts + keys_here)
    base = jnp.sum(jnp.where(in_block, starts, 0), axis=0, keepdims=True)
    local = sel - base
    lanes = lax.broadcasted_iota(jnp.int32, (keys_here, top_count), 0)
    mask = dot_nt(
        in_block.astype(jnp.float32).astype(jnp.bfloat16),
        (local == lanes).astype(jnp.float32).astype(jnp.bfloat16),
    )
    for d in range(n):
        mask_ref[0, d] = mask[d : d + 1]
    to_twin(0).start()

    def attend(which, blocks, fresh=False):
        pieces = []
        for slot, owner in blocks:
            s = jnp.dot(q_both[which], kv[slot], preferred_element_type=jnp.float32) * score_scale
            pieces.append(jnp.where(mask_ref[which, owner] > 0.5, s, floor_value))
        peak = functools.reduce(
            jnp.maximum, [jnp.max(s, axis=1, keepdims=True) for s in pieces]
        )
        if not fresh:
            before = m_ref[which]
            peak = jnp.maximum(before, peak)
            fade = jnp.exp(before - peak)
        total = None
        mixed = None
        for s, (slot, owner) in zip(pieces, blocks):
            expo = jnp.exp(s - peak)
            summed = jnp.sum(expo, axis=1, keepdims=True)
            product = dot_nt(expo.astype(jnp.bfloat16), kv[slot, :LATENT, :])
            total = summed if total is None else total + summed
            mixed = product if mixed is None else mixed + product
        if not fresh:
            total = total + fade * l_ref[which]
            mixed = mixed + fade * acc_ref[which]
        return peak, total, mixed

    def attend_store(which, blocks, fresh=False):
        peak, total, mixed = attend(which, blocks, fresh)
        m_ref[which] = peak
        l_ref[which] = total
        acc_ref[which] = mixed

    here = [(0, me)]
    near = [(1, mate_x), (2, mate_z)]
    last = [(3, diagonal)]

    load(5).wait()
    attend_store(0, here, True)

    for i in range(PIECES):
        for axis, k in ((0, x_order[i]), (1, z_order[i])):
            own(axis, k).wait_recv()
            if (axis == 1) == (k < RELAY_X):
                relay(k).start()
            swap(1 + axis, k).start()


    @pl.when(jnp.logical_not(early))
    def _():
        to_twin(1).start()

    to_twin(0).wait_recv()
    for o in range(3):
        row_copy(o).wait_recv()

    def stats(which, owner):
        scores = jnp.concatenate(
            [row_recv[d, pl.ds(owner // ring, 1)][0] for d in range(ring)], axis=0
        )
        chosen = jnp.concatenate([mask_ref[which, first + d] for d in range(ring)], axis=0)
        places = (lax.broadcasted_iota(jnp.int32, scores.shape, 0) + first) * keys_here
        places = places + lax.broadcasted_iota(jnp.int32, scores.shape, 1)
        position = n * keys_here - pb_total * per_block + pb * per_block + owner
        found = []
        for keep in (places <= position, chosen > 0.5):
            kept = jnp.where(keep, scores, floor_value)
            top = jnp.max(jnp.max(kept, axis=1, keepdims=True), axis=0, keepdims=True)
            terms = jnp.where(keep, jnp.exp(kept - top), 0.0)
            summed = jnp.sum(jnp.sum(terms, axis=1, keepdims=True), axis=0, keepdims=True)
            found += [top, summed]
        return found

    spots = lax.broadcasted_iota(jnp.int32, share_send.shape, 1)
    packed = jnp.zeros(share_send.shape, jnp.float32)
    for at, value in enumerate(stats(0, me) + stats(1, twin)):
        packed = jnp.where(spots == at, value, packed)
    share_send[...] = packed
    share_recv[me] = packed
    pl.semaphore_wait(entered, 1)
    for o in range(1, n):
        share_copy(o).start()

    square = (HEADS, HEADS)
    eye = lax.broadcasted_iota(jnp.int32, square, 0) == lax.broadcasted_iota(jnp.int32, square, 1)

    def as_row(column):
        return jnp.sum(jnp.where(eye, column, 0.0), axis=0, keepdims=True)

    def as_column(row):
        return jnp.sum(jnp.where(eye, row, 0.0), axis=1, keepdims=True)

    def last_arrives():
        for k in range(PIECES):
            relay(k).wait_recv()
            swap(3, k).start()

    def give_part(peak, total, mixed):
        part_send[...] = (mixed / total).astype(jnp.bfloat16)
        to_twin(3).start()
        stat_send[...] = jnp.concatenate([as_row(peak), as_row(total)], axis=0)
        to_twin(2).start()

    def twin_arrives():
        to_twin(1).wait_recv()

    @pl.when(serves_early)
    def _():
        last_arrives()
        twin_arrives()
        swap_wait(1)
        swap_wait(2)
        attend_store(1, here + near, True)
        swap_wait(3)
        give_part(*attend(1, last))
        attend_store(0, near)
        attend_store(0, last)

    @pl.when(jnp.logical_not(serves_early))
    def _():
        last_arrives()
        swap_wait(1)
        swap_wait(2)
        attend_store(0, near)
        swap_wait(3)
        attend_store(0, last)
        twin_arrives()
        give_part(*attend(1, here + near + last, True))

    peak, total, mixed = m_ref[0], l_ref[0], acc_ref[0]
    to_twin(2).wait_recv()
    other_peak = as_column(stat_recv[0:1])
    other_total = as_column(stat_recv[1:2])
    top = jnp.maximum(peak, other_peak)
    scale = jnp.exp(peak - top)
    other = jnp.exp(other_peak - top) * other_total
    whole = scale * total + other
    mixed = mixed * (scale / whole)
    other = other / whole
    to_twin(3).wait_recv()
    result = mixed + other * part_recv[...].astype(jnp.float32)
    spans = LATENT // LANES
    for odd in range(2):
        for g in range(spans):
            out_ref[pl.ds(odd * spans + g, pairs, stride=2 * spans), :] = result[
                odd * pairs : (odd + 1) * pairs, g * LANES : (g + 1) * LANES
            ]

    for o in range(1, n):
        share_copy(o).wait_recv()
    table = jnp.concatenate([share_recv[d] for d in range(n)], axis=0)
    across = jnp.concatenate([table[ring:], table[:ring]], axis=0)

    def merged(at):
        top_a, sum_a = table[:, at : at + 1], table[:, at + 1 : at + 2]
        top_b, sum_b = across[:, at + 4 : at + 5], across[:, at + 5 : at + 6]
        top = jnp.maximum(top_a, top_b)
        return top + jnp.log(jnp.exp(top_a - top) * sum_a + jnp.exp(top_b - top) * sum_b)

    share = merged(2) - merged(0)
    corner = (n, share_ref.shape[1])
    level = lax.broadcasted_iota(jnp.int32, corner, 0) == lax.broadcasted_iota(
        jnp.int32, corner, 1
    )
    share_ref[...] = jnp.sum(jnp.where(level, share, 0.0), axis=0, keepdims=True)

    for o in range(3):
        row_copy(o).wait_send()
    for o in range(1, n):
        share_copy(o).wait_send()
    for j in range(4):
        to_twin(j).wait_send()
    for k in range(PIECES):
        own(0, k).wait_send()
        own(1, k).wait_send()
        relay(k).wait_send()
        for slot in (1, 2, 3):
            swap(slot, k).wait_send()


def square_call(n, pb_total, operands):
    att_query, latent, index_query, index_weight, index_keys, selected = operands
    row_width, keys_here = latent.shape
    per_block = index_query.shape[0]
    vmem = pl.BlockSpec(memory_space=pltpu.VMEM)
    dma = pltpu.SemaphoreType.DMA
    return pl.pallas_call(
        functools.partial(square_kernel, n, pb_total),
        out_shape=(
            pltpu.VMEM((HEADS * LATENT // LANES, LANES), jnp.float32),
            pltpu.VMEM((1, per_block), jnp.float32),
        ),
        in_specs=[pl.BlockSpec(memory_space=pl.ANY)] * 6,
        out_specs=(vmem, vmem),
        scratch_shapes=[
            pltpu.VMEM(att_query.shape, att_query.dtype),
            pltpu.VMEM(index_query.shape, index_query.dtype),
            pltpu.VMEM(index_weight.shape, index_weight.dtype),
            pltpu.VMEM(index_keys.shape, index_keys.dtype),
            pltpu.VMEM(selected.shape, selected.dtype),
            pltpu.VMEM((n // 2, row_width, keys_here), jnp.bfloat16),
            pltpu.VMEM((n // 2, 2, 1, keys_here), jnp.float32),
            pltpu.VMEM((n // 2, 2, 1, keys_here), jnp.float32),
            pltpu.VMEM((1, LANES), jnp.float32),
            pltpu.VMEM((n, 1, LANES), jnp.float32),
            pltpu.VMEM((2, n, 1, keys_here), jnp.float32),
            pltpu.VMEM((2, HEADS, 1), jnp.float32),
            pltpu.VMEM((2, HEADS, 1), jnp.float32),
            pltpu.VMEM((2, HEADS, LATENT), jnp.float32),
            pltpu.VMEM((HEADS * row_width // LANES, LANES), jnp.float32),
            pltpu.VMEM((2, HEADS, row_width), jnp.bfloat16),
            pltpu.VMEM((HEADS, LATENT), jnp.bfloat16),
            pltpu.VMEM((HEADS, LATENT), jnp.bfloat16),
            pltpu.VMEM((2, HEADS), jnp.float32),
            pltpu.VMEM((2, HEADS), jnp.float32),
            dma((6,)),
            dma((2, PIECES)),
            dma((PIECES,)),
            dma((3, PIECES)),
            dma((3, PIECES)),
            dma((3, PIECES)),
            dma((3,)),
            dma((3,)),
            dma((n,)),
            dma((n,)),
            dma((4,)),
            dma((4,)),
            pltpu.SemaphoreType.REGULAR,
        ],
        compiler_params=pltpu.CompilerParams(collective_id=0, has_side_effects=True),
        name="sparse_prefill",
    )(*operands)


def ring_call(n, pb_total, operands):
    half = n // 4
    latent, per_block = operands[1], operands[2].shape[0]
    row_width, keys_here = latent.shape
    vmem = pl.BlockSpec(memory_space=pltpu.VMEM)
    dma = pltpu.SemaphoreType.DMA
    return pl.pallas_call(
        functools.partial(kernel, n, pb_total),
        out_shape=(
            pltpu.VMEM((HEADS * LATENT // LANES, LANES), jnp.bfloat16),
            pltpu.VMEM((1, per_block), jnp.float32),
        ),
        in_specs=[vmem, pl.BlockSpec(memory_space=pl.ANY), vmem, vmem, vmem, vmem],
        out_specs=(vmem, vmem),
        scratch_shapes=[
            pltpu.VMEM((half + 1, row_width, keys_here), jnp.bfloat16),
            pltpu.VMEM((half, row_width, keys_here), jnp.bfloat16),
            pltpu.VMEM((per_block, 1, keys_here), jnp.float32),
            pltpu.VMEM((n, 1, keys_here), jnp.float32),
            pltpu.VMEM((1, 128), jnp.float32),
            pltpu.VMEM((n, 1, 128), jnp.float32),
            pltpu.VMEM((2, n, 1, keys_here), jnp.float32),
            pltpu.VMEM((2, HEADS, 1), jnp.float32),
            pltpu.VMEM((2, HEADS, 1), jnp.float32),
            pltpu.VMEM((2, HEADS, LATENT), jnp.float32),
            pltpu.VMEM((HEADS * row_width // LANES, LANES), jnp.float32),
            pltpu.VMEM((HEADS * LATENT // LANES, LANES), jnp.float32),
            pltpu.VMEM((2, HEADS, row_width), jnp.bfloat16),
            pltpu.VMEM((HEADS, LATENT), jnp.bfloat16),
            pltpu.VMEM((HEADS, LATENT), jnp.bfloat16),
            pltpu.VMEM((2, HEADS), jnp.float32),
            pltpu.VMEM((2, HEADS), jnp.float32),
            dma,
            dma((2, half + 1, CHUNKS)),
            dma((2, half + 1, CHUNKS)),
            dma((2, half + 1, CHUNKS)),
            dma((2, half + 1, CHUNKS)),
            dma((n,)),
            dma((n,)),
            dma((n,)),
            dma((n,)),
            dma((4,)),
            dma((4,)),
            pltpu.SemaphoreType.REGULAR((half,)),
        ],
        compiler_params=pltpu.CompilerParams(collective_id=0, has_side_effects=True),
        name="sparse_prefill",
    )(*operands)


def finish(rows_ref, shares_ref, out_ref, share_ref):
    flat = rows_ref[...].astype(jnp.float32).reshape(1, HEADS * LATENT)
    out_ref[0] = flat.astype(jnp.bfloat16)
    share_ref[...] = shares_ref[...]


def body(n, pb_total, att_query, latent_cache, index_query, index_weight, index_keys, selected):
    per_block = index_query.shape[1]
    operands = (
        att_query,
        latent_cache.T,
        index_query[0],
        index_weight[0],
        index_keys,
        selected[0],
    )
    call = square_call if n == 8 else ring_call
    results = [
        pltpu.with_memory_space_constraint(r, pltpu.VMEM) for r in call(n, pb_total, operands)
    ]
    vmem = pl.BlockSpec(memory_space=pltpu.VMEM)
    return pl.pallas_call(
        finish,
        out_shape=(
            jax.ShapeDtypeStruct((1, 1, HEADS * LATENT), jnp.bfloat16),
            jax.ShapeDtypeStruct((1, per_block), jnp.float32),
        ),
        in_specs=[vmem, vmem],
        out_specs=(vmem, vmem),
        name="finish",
    )(*results)


def solution(mesh):
    return jax.shard_map(
        functools.partial(body, mesh.shape["ctx"], mesh.shape["pb"]),
        mesh=mesh,
        in_specs=(
            P(("groups", "pb"), "ctx", None),
            P(("groups", "ctx"), None),
            P(("groups", "pb"), None, None),
            P(("groups", "pb"), None, None),
            P(("groups", "ctx"), None),
            P(("groups", "pb"), "ctx", None),
        ),
        out_specs=(P(("groups", "pb"), "ctx", None), P(("groups", "pb"), None)),
        check_vma=False,
    )
```
